128 devices in a mesh: plane: 64 (over x, y, z), cuts: 2 (over core).
Axes of the slice: x: 4, y: 4, z: 4, core: 2. Of those that a mesh axis runs over, the one named last changes fastest.
Arguments:
- image: float32 [1024, 128, 256], P('plane', None, 'cuts'), may hold values from 0 to 2
- projection_weight_tiles: bfloat16 [6144, 256, 256], P('plane'), may hold values from -0.0390625 to 0.0390625
- pair_tile_index: int32 [6144], P('plane'), may hold values from 0 to 7
- pair_ray_block: int32 [6144], P('plane'), may hold values from 0 to 63
- ray_owner: int32 [64], replicated, may hold values from 0 to 63, each once
- active_pair_count: int32 [64], P('plane'), may hold values from 12 to 96, as said below
- measured: float32 [64, 256, 256], P('plane', None, 'cuts'), may hold values from -6 to 6
Outputs:
- volume: float32 [1024, 128, 256], P('plane', None, 'cuts')
- residual: bfloat16 [64, 256, 256], P('plane', None, 'cuts')
The draws below stay inside these ranges and needn't reach their ends.
Inputs may be any that keep to these rules, and one draw needn't show every extreme that they name: The first active_pair_count[d] pairs of plane index d are live and the rest are not; some index has all 96 pairs live. `ray_owner`: each owner position is taken by exactly one ray block.
All inputs are finite; a program needn't handle non-finite values.
Results may differ from the reference program's by a relative error of at most 0.0045.
Values may be sent and summed in bfloat16 or wider, within the bound.
A program may use at most 128 MiB of HBM per device.

```python
import jax
import jax.numpy as jnp
from jax import lax

TILE = 16
RAYS_PER_BLOCK = 256
COLS = 128
PAIRS_PER_PLANE = 96
SWEEPS = 4
NDEV = 64
TILE_VOXELS = 256
NY = 1024
SLICES = 256
TILES_PER_PLANE = 8
NTILES = 512
RAY_BLOCK_TOTAL = 64
PAIR_TOTAL = 6144


def draw_active_pair_count(key, part):
    first_key = jax.random.fold_in(key, 11)
    second_key = jax.random.fold_in(key, 23)
    counts_drawn = jax.random.randint(first_key, (NDEV,), PAIRS_PER_PLANE // 8, PAIRS_PER_PLANE + 1)
    busiest = jax.random.randint(second_key, (), 0, NDEV)
    return jnp.where(jnp.arange(NDEV) == busiest, PAIRS_PER_PLANE, counts_drawn).astype(jnp.int32)


def with_ends(drawn, key, low, high):
    longest = drawn.shape.index(max(drawn.shape))
    spots = []
    for shift in (0, 1):
        where = [jax.random.randint(jax.random.fold_in(key, axis), (), 0, length) for axis, length in enumerate(drawn.shape)]
        where[longest] = (where[longest] + shift) % drawn.shape[longest]
        spots.append(tuple(where))
    return drawn.at[spots[0]].set(low).at[spots[1]].set(high)


def levels(rng, shape, cuts, least, top_value):
    gain = 1.0
    for dim, parts in cuts:
        heights = jax.random.uniform(jax.random.fold_in(jax.random.fold_in(rng, 6), dim), (parts,), jnp.float32, least / len(cuts), top_value / len(cuts))
        gain = gain * jnp.repeat(jnp.exp(heights), shape[dim] // parts).reshape((-1,) + (1,) * (len(shape) - 1 - dim))
    return gain


def scatter_about(rng, shape, scale, most, shards=(), kind=jnp.bfloat16):
    gain = levels(rng, shape, shards, -0.22, 0.18) if shards else 1.0
    values = jax.random.normal(rng, shape, jnp.float32) * scale * gain
    return jnp.minimum(jnp.maximum(values, -most), most).astype(kind)


def setup_inputs(seed: int = 0) -> dict:
    arg_keys = jax.random.split(jax.random.key(seed), 8)
    return {
        "image": jnp.clip(2.0 * jax.random.uniform(arg_keys[0], (NY, COLS, SLICES), jnp.float32) ** levels(arg_keys[0], (NY, COLS, SLICES), ((0, 64), (2, 2)), -0.2, 0.2), 0.0, 2.0),
        "projection_weight_tiles": scatter_about(arg_keys[1], (PAIR_TOTAL, TILE_VOXELS, RAYS_PER_BLOCK), (TILE_VOXELS * PAIRS_PER_PLANE) ** -0.5, 0.0390625, ((0, 64),)),
        "pair_tile_index": with_ends(jax.random.randint(arg_keys[2], (PAIR_TOTAL,), 0, TILES_PER_PLANE), jax.random.fold_in(arg_keys[2], 1), 0, TILES_PER_PLANE - 1).astype(jnp.int32),
        "pair_ray_block": with_ends(jax.random.randint(arg_keys[3], (PAIR_TOTAL,), 0, RAY_BLOCK_TOTAL), jax.random.fold_in(arg_keys[3], 1), 0, RAY_BLOCK_TOTAL - 1).astype(jnp.int32),
        "ray_owner": jax.random.permutation(arg_keys[4], RAY_BLOCK_TOTAL).astype(jnp.int32),
        "active_pair_count": draw_active_pair_count(jax.random.fold_in(arg_keys[7], 71), 0),
        "measured": scatter_about(arg_keys[6], (RAY_BLOCK_TOTAL, RAYS_PER_BLOCK, SLICES), 1.0, 6.0, ((0, 64), (2, 2)), jnp.float32),
    }


smooth_square = 0.09
flow_step = 0.04
relax_step = 4.0

def smooth_sweep(volume, inside):
    rise_rows = jnp.concatenate([volume[1:] - volume[:-1], -volume[-1:]], axis=0)
    rise_cols = jnp.concatenate([volume[:, 1:] - volume[:, :-1], -volume[:, -1:]], axis=1)
    rise_slices = jnp.concatenate([volume[:, :, 1:] - volume[:, :, :-1], -volume[:, :, -1:]], axis=2)
    length = jnp.sqrt(smooth_square + rise_rows * rise_rows + rise_cols * rise_cols + rise_slices * rise_slices)
    flow_rows = rise_rows / length * inside
    flow_cols = rise_cols / length * inside
    flow_slices = rise_slices / length * inside
    diverge = flow_rows - jnp.concatenate([jnp.zeros_like(flow_rows[:1]), flow_rows[:-1]], axis=0)
    diverge = diverge + flow_cols - jnp.concatenate([jnp.zeros_like(flow_cols[:, :1]), flow_cols[:, :-1]], axis=1)
    diverge = diverge + flow_slices - jnp.concatenate([jnp.zeros_like(flow_slices[:, :, :1]), flow_slices[:, :, :-1]], axis=2)
    return (volume + flow_step * diverge) * inside

def reference(image, projection_weight_tiles, pair_tile_index, pair_ray_block, ray_owner, active_pair_count, measured):
    grouped = image.reshape(NY // TILE, TILE, COLS // TILE, TILE, SLICES).transpose(0, 2, 1, 3, 4).reshape(NTILES, TILE_VOXELS, SLICES)
    rounded = lax.optimization_barrier(grouped.astype(jnp.bfloat16)).astype(jnp.float32)
    plane_index_of = (jnp.arange(PAIR_TOTAL, dtype=jnp.int32) // PAIRS_PER_PLANE).astype(jnp.int32)
    owner_of = ray_owner[pair_ray_block].astype(jnp.int32)
    active_pair = (jnp.arange(PAIR_TOTAL, dtype=jnp.int32) % PAIRS_PER_PLANE < active_pair_count[plane_index_of]).astype(jnp.float32)
    stacked = (projection_weight_tiles.reshape(NDEV, PAIRS_PER_PLANE, TILE_VOXELS, RAYS_PER_BLOCK), pair_tile_index.reshape(NDEV, PAIRS_PER_PLANE), owner_of.reshape(NDEV, PAIRS_PER_PLANE), active_pair.reshape(NDEV, PAIRS_PER_PLANE), rounded.reshape(NDEV, TILES_PER_PLANE, TILE_VOXELS, SLICES))

    def forward(running, pieces):
        weights, tile_ids, owners, live_part, local_tiles = pieces
        values = local_tiles[tile_ids]
        product = jnp.einsum('svr,svc->src', weights.astype(jnp.float32), values, precision=lax.Precision.HIGHEST)
        product = product * live_part[:, None, None]
        return (running + jax.ops.segment_sum(product, owners, num_segments=RAY_BLOCK_TOTAL), None)
    projection, unused = lax.scan(forward, jnp.zeros((RAY_BLOCK_TOTAL, RAYS_PER_BLOCK, SLICES), jnp.float32), stacked)
    mismatch = measured - projection
    residual = (mismatch / jnp.sqrt(1.0 + mismatch * mismatch)).astype(jnp.bfloat16)
    residual_wide = residual.astype(jnp.float32)

    def backward(carry, pieces):
        weights, tile_ids, owners, live_part, local_tiles = pieces
        product = jnp.einsum('svr,src->svc', weights.astype(jnp.float32), residual_wide[owners], precision=lax.Precision.HIGHEST)
        product = product * live_part[:, None, None]
        return (carry, jax.ops.segment_sum(product, tile_ids, num_segments=TILES_PER_PLANE))
    unused, update = lax.scan(backward, jnp.zeros((), jnp.float32), stacked)
    update = update.reshape(NY // TILE, COLS // TILE, TILE, TILE, SLICES).transpose(0, 2, 1, 3, 4).reshape(NY, COLS, SLICES)
    volume = jnp.maximum(image + relax_step * update, 0.0)
    inside = jnp.ones((1, 1, 1), jnp.float32)
    for repeat in range(SWEEPS):
        volume = smooth_sweep(volume, inside)
    return (volume, residual)
```

```python
import functools

import jax
import jax.numpy as jnp
from jax import lax
from jax.experimental import pallas as pl
from jax.experimental.pallas import tpu as pltpu
from jax.sharding import PartitionSpec as P

TILE = 16
SWEEPS = 4
smooth_square = 0.09
flow_step = 0.04
relax_step = 4.0

SIDE = 4
GROUP = 8
HALO = 4
VMEM_LIMIT = 60 * 1024 * 1024
ORDERS = ((0, 1, 2), (1, 2, 0), (2, 0, 1))
SUM_ROWS = ((0, 48), (48, 48), (96, 32))
SPREAD_ROWS = ((0, 96), (96, 80), (176, 80))

F32 = jnp.float32
BF16 = jnp.bfloat16


def coordinates():
    here = lax.axis_index("plane")
    return here // (SIDE * SIDE), (here // SIDE) % SIDE, here % SIDE


def relative_slot(owner):
    x, y, z = coordinates()
    dx = lax.bitwise_and(owner // (SIDE * SIDE) - x + SIDE, SIDE - 1)
    dy = lax.bitwise_and((owner // SIDE) % SIDE - y + SIDE, SIDE - 1)
    dz = lax.bitwise_and(owner % SIDE - z + SIDE, SIDE - 1)
    return (dx * SIDE + dy) * SIDE + dz


def forward_kernel(tiles, blocks, owners, count, image, weights, out, voxels, sums):
    step = pl.program_id(0)
    slots = sums.shape[0] - 1

    @pl.when(step == 0)
    def _():
        for tile in range(voxels.shape[0]):
            piece = image[:, tile * TILE : (tile + 1) * TILE, :]
            voxels[tile] = piece.reshape(TILE * TILE, piece.shape[-1]).T.astype(BF16)

        def clear(i, c):
            sums[i] = jnp.zeros(sums.shape[1:], F32)
            return c

        lax.fori_loop(0, slots, clear, 0)

    for i in range(GROUP):
        pair = step * GROUP + i
        slot = jnp.where(pair < count[0], relative_slot(owners[blocks[pair]]), slots)
        product = jnp.dot(voxels[tiles[pair]], weights[i], preferred_element_type=F32)
        sums[slot, 0] += product[:, :128]
        sums[slot, 1] += product[:, 128:]

    @pl.when(step == pl.num_programs(0) - 1)
    def _():
        def finish(i, c):
            out[i] = sums[i].astype(BF16)
            return c

        lax.fori_loop(0, slots, finish, 0)


def forward(tiles, blocks, owners, count, image, weights):
    pairs, voxels, rays = weights.shape
    rows, cols, slices = image.shape
    slots = owners.shape[0]
    tile_count = cols // TILE
    return pl.pallas_call(
        forward_kernel,
        out_shape=jax.ShapeDtypeStruct((slots, 2, slices, 128), BF16),
        grid_spec=pltpu.PrefetchScalarGridSpec(
            num_scalar_prefetch=4,
            grid=(pairs // GROUP,),
            in_specs=[
                pl.BlockSpec((rows, cols, slices), lambda i, *_: (0, 0, 0)),
                pl.BlockSpec((GROUP, voxels, rays), lambda i, *_: (i, 0, 0)),
            ],
            out_specs=pl.BlockSpec((slots, 2, slices, 128), lambda i, *_: (0, 0, 0, 0)),
            scratch_shapes=[
                pltpu.VMEM((tile_count, slices, voxels), BF16),
                pltpu.VMEM((slots + 1, 2, slices, 128), F32),
            ],
        ),
        compiler_params=pltpu.CompilerParams(vmem_limit_bytes=VMEM_LIMIT),
        name="project",
    )(tiles, blocks, owners, count, image, weights)


def backward_kernel(tiles, blocks, owners, count, image, spread, weights, out, sums):
    step = pl.program_id(0)
    tile_count = sums.shape[0] - 1

    @pl.when(step == 0)
    def _():
        for i in range(tile_count):
            sums[i] = jnp.zeros(sums.shape[1:], F32)

    for i in range(GROUP):
        pair = step * GROUP + i
        tile = jnp.where(pair < count[0], tiles[pair], tile_count)
        slot = relative_slot(owners[blocks[pair]])
        sums[tile] += jnp.dot(weights[i], spread[slot], preferred_element_type=F32)

    @pl.when(step == pl.num_programs(0) - 1)
    def _():
        def finish(row, c):
            start = pl.multiple_of(row * TILE, TILE)
            update = jnp.concatenate(
                [sums[tile, pl.ds(start, TILE), :] for tile in range(tile_count)], axis=0
            )
            out[row] = jnp.maximum(image[row] + relax_step * update, 0.0).T
            return c

        lax.fori_loop(0, image.shape[0], finish, 0)


def backward(tiles, blocks, owners, count, image, spread, weights):
    pairs, voxels, rays = weights.shape
    rows, cols, slices = image.shape
    slots = owners.shape[0]
    return pl.pallas_call(
        backward_kernel,
        out_shape=jax.ShapeDtypeStruct((rows, slices, cols), F32),
        grid_spec=pltpu.PrefetchScalarGridSpec(
            num_scalar_prefetch=4,
            grid=(pairs // GROUP,),
            in_specs=[
                pl.BlockSpec((rows, cols, slices), lambda i, *_: (0, 0, 0)),
                pl.BlockSpec((slots, rays, slices), lambda i, *_: (0, 0, 0)),
                pl.BlockSpec((GROUP, voxels, rays), lambda i, *_: (i, 0, 0)),
            ],
            out_specs=pl.BlockSpec((rows, slices, cols), lambda i, *_: (0, 0, 0)),
            scratch_shapes=[pltpu.VMEM((cols // TILE + 1, voxels, slices), F32)],
        ),
        compiler_params=pltpu.CompilerParams(vmem_limit_bytes=VMEM_LIMIT),
        name="backproject",
    )(tiles, blocks, owners, count, image, spread, weights)


def neighbour(dim, shift):
    place = list(coordinates())
    place[dim] = (place[dim] + shift + SIDE) % SIDE
    return (place[0] * SIDE + place[1]) * SIDE + place[2]


def pick(order, *where):
    index = [slice(None)] * 3
    for position, value in enumerate(where):
        index[ORDERS[order][position]] = value
    return tuple(index)


def exchange_kernel(
    partial, measured, residual, spread_out, part, total, own, gather, *rest
):
    opposite = [rest[3 * o : 3 * o + 3] for o in range(3)]
    direct = [rest[9 + 3 * o : 12 + 3 * o] for o in range(3)]
    sum_send, sum_recv, spread_send, spread_recv, local = rest[18:]

    barrier = pltpu.get_barrier_semaphore()
    for dim in range(3):
        for shift in (1, -1):
            pl.semaphore_signal(barrier, inc=1, device_id={"plane": neighbour(dim, shift)})
    load = pltpu.make_async_copy(partial, part, local.at[0])
    load.start()
    load.wait()
    pl.semaphore_wait(barrier, 6)

    def source(order, phase, j, half):
        first, rows = SUM_ROWS[order]
        if phase == 2:
            return total[order].at[j, half]
        return part.at[pick(order, *([0] * phase), j) + (half, pl.ds(first, rows))]

    def send_sum(order, phase, slot, src, dst, shift):
        number = (order * 3 + phase) * 6 + slot
        copy = pltpu.make_async_remote_copy(
            src_ref=src,
            dst_ref=dst,
            send_sem=sum_send.at[number],
            recv_sem=sum_recv.at[number],
            device_id={"plane": neighbour(ORDERS[order][phase], shift)},
        )
        copy.start()
        return copy

    def combine(phase, target, first, *others):
        if phase == 0:

            def body(i, c):
                for k in range(SIDE):
                    value = first[i, k].astype(F32)
                    for other in others:
                        value = value + other[i, k].astype(F32)
                    target[i, k] = value.astype(target.dtype)
                return c

            lax.fori_loop(0, SIDE, body, 0)
        elif phase == 1:
            for k in range(SIDE):
                value = first[k].astype(F32)
                for other in others:
                    value = value + other[k].astype(F32)
                target[k] = value.astype(target.dtype)
        else:
            value = first[...]
            for other in others:
                value = value + other[...]
            target[...] = value

    sends = []
    for phase in range(3):
        early = {}
        for order in range(3):
            opp, dirs = opposite[order][phase], direct[order][phase]
            early[order] = [
                send_sum(order, phase, 0, source(order, phase, 2, 0), opp.at[0], 1),
                send_sum(order, phase, 1, source(order, phase, 2, 1), opp.at[1], -1),
                send_sum(order, phase, 2, source(order, phase, 1, 1), dirs.at[0, 1], 1),
                send_sum(order, phase, 3, source(order, phase, 3, 0), dirs.at[1, 0], -1),
            ]
        late = {}
        for order in range(3):
            opp, dirs = opposite[order][phase], direct[order][phase]
            early[order][0].wait_recv()
            here = source(order, phase, 1, 0)
            combine(phase, here, here, opp.at[0])
            a = send_sum(order, phase, 4, here, dirs.at[0, 0], 1)
            early[order][1].wait_recv()
            here = source(order, phase, 3, 1)
            combine(phase, here, here, opp.at[1])
            b = send_sum(order, phase, 5, here, dirs.at[1, 1], -1)
            late[order] = [a, b]
        for order in range(3):
            dirs = direct[order][phase]
            for copy in early[order][2:] + late[order]:
                copy.wait_recv()
            first, rows = SUM_ROWS[order]
            for half in range(2):
                here = source(order, phase, 0, half)
                if phase == 0:
                    target = here
                elif phase == 1:
                    target = total[order].at[:, half]
                else:
                    target = own.at[half, pl.ds(first, rows)]
                combine(phase, target, here, dirs.at[0, half], dirs.at[1, half])
            sends += early[order] + late[order]

    for half in range(2):
        rows = pl.ds(half * 128, 128)
        mismatch = measured[0, rows, :] - own[half].T
        value = (mismatch * lax.rsqrt(1.0 + mismatch * mismatch)).astype(BF16)
        residual[0, rows, :] = value
        gather[0, 0, 0, rows, :] = value

    def send_spread(order, phase, slot, src, dst, shift):
        number = (order * 3 + phase) * 4 + slot
        copy = pltpu.make_async_remote_copy(
            src_ref=src,
            dst_ref=dst,
            send_sem=spread_send.at[number],
            recv_sem=spread_recv.at[number],
            device_id={"plane": neighbour(ORDERS[order][phase], shift)},
        )
        copy.start()
        return copy

    def held(order, phase, j, first, rows):
        return gather.at[pick(order, *([0] * phase), j) + (pl.ds(first, rows),)]

    for phase in (2, 1, 0):
        early = {}
        for order in range(3):
            first, rows = SPREAD_ROWS[order]
            mine = held(order, phase, 0, first, rows)
            early[order] = [
                send_spread(order, phase, 0, mine, held(order, phase, 3, first, rows), 1),
                send_spread(order, phase, 1, mine, held(order, phase, 1, first, rows), -1),
            ]
        late = []
        for order in range(3):
            first, rows = SPREAD_ROWS[order]
            cut = 48
            early[order][0].wait_recv()
            a = send_spread(
                order, phase, 2, held(order, phase, 3, first, cut), held(order, phase, 2, first, cut), 1
            )
            early[order][1].wait_recv()
            first, rows = first + cut, rows - cut
            b = send_spread(
                order, phase, 3, held(order, phase, 1, first, rows), held(order, phase, 2, first, rows), -1
            )
            late += [a, b]
        for copy in late:
            copy.wait_recv()
        for order in range(3):
            sends += early[order]
        sends += late

    store = pltpu.make_async_copy(gather, spread_out, local.at[1])
    store.start()
    for copy in sends:
        copy.wait_send()
    store.wait()


def exchange(partial, measured):
    slots, halves, slices, lanes = partial.shape
    rays = measured.shape[1]
    cube = (SIDE, SIDE, SIDE)
    opposite, direct = [], []
    for order in range(3):
        rows = SUM_ROWS[order][1]
        for phase, (blocks, kind) in enumerate((((SIDE, SIDE), BF16), ((SIDE,), BF16), ((), F32))):
            opposite.append(pltpu.VMEM((2, *blocks, rows, lanes), kind))
            direct.append(pltpu.VMEM((2, 2, *blocks, rows, lanes), kind))

    def kernel(partial, measured, residual, spread_out, part, t0, t1, t2, own, gather, *rest):
        exchange_kernel(
            partial, measured, residual, spread_out, part, (t0, t1, t2), own, gather, *rest
        )

    residual, spread = pl.pallas_call(
        kernel,
        out_shape=(
            jax.ShapeDtypeStruct((1, rays, slices), BF16),
            jax.ShapeDtypeStruct((*cube, rays, slices), BF16),
        ),
        in_specs=[
            pl.BlockSpec(memory_space=pl.ANY),
            pl.BlockSpec(memory_space=pltpu.VMEM),
        ],
        out_specs=(pl.BlockSpec(memory_space=pltpu.VMEM), pl.BlockSpec(memory_space=pl.ANY)),
        scratch_shapes=[
            pltpu.VMEM((*cube, halves, slices, lanes), BF16),
            *[pltpu.VMEM((SIDE, halves, SUM_ROWS[o][1], lanes), F32) for o in range(3)],
            pltpu.VMEM((halves, slices, lanes), F32),
            pltpu.VMEM((*cube, rays, slices), BF16),
            *opposite,
            *direct,
            pltpu.SemaphoreType.DMA((54,)),
            pltpu.SemaphoreType.DMA((54,)),
            pltpu.SemaphoreType.DMA((36,)),
            pltpu.SemaphoreType.DMA((36,)),
            pltpu.SemaphoreType.DMA((2,)),
        ],
        compiler_params=pltpu.CompilerParams(
            collective_id=0, has_side_effects=True, vmem_limit_bytes=VMEM_LIMIT
        ),
        name="exchange",
    )(partial.reshape(*cube, halves, slices, lanes), measured)
    return residual, spread.reshape(slots, rays, slices)


def sweep_kernel(relaxed, out, field, other, flux_rows, flux_slices, edge, side, corner, *sems):
    row_send, row_recv, side_send, side_recv = sems
    rows, slices, cols = relaxed.shape
    here = lax.axis_index("plane")
    cut = lax.axis_index("cuts")
    last = lax.axis_size("plane") - 1
    up = (here + last) % (last + 1)
    down = (here + 1) % (last + 1)
    base = 8 + 8 * cut

    barrier = pltpu.get_barrier_semaphore()
    for plane in (up, down):
        for core in (0, 1):
            pl.semaphore_signal(barrier, inc=1, device_id={"plane": plane, "cuts": core})
    pl.semaphore_signal(barrier, inc=1, device_id={"plane": here, "cuts": 1 - cut})
    pl.semaphore_wait(barrier, 5)

    edge[0] = relaxed[rows - HALO :].astype(BF16)
    edge[1] = relaxed[:HALO].astype(BF16)
    start = pl.multiple_of(120 * (1 - cut), 8)
    side[0] = relaxed[:, pl.ds(start, 8), :]
    copies = []

    def send(src, dst, plane, core, number, which):
        copy = pltpu.make_async_remote_copy(
            src_ref=src,
            dst_ref=dst,
            send_sem=which[0].at[number],
            recv_sem=which[1].at[number],
            device_id={"plane": plane, "cuts": core},
        )
        copy.start()
        copies.append(copy)

    send(side.at[0], side.at[1], here, 1 - cut, 0, (side_send, side_recv))
    send(side.at[0, pl.ds(rows - HALO, HALO)], corner.at[0], down, 1 - cut, 1, (side_send, side_recv))
    send(side.at[0, pl.ds(0, HALO)], corner.at[1], up, 1 - cut, 2, (side_send, side_recv))
    send(edge.at[0], edge.at[2], down, cut, 0, (row_send, row_recv))
    send(edge.at[1], edge.at[3], up, cut, 1, (row_send, row_recv))

    total = rows + 2 * HALO
    zero = jnp.zeros((8, cols), F32)
    chunks = (slices + 8) // 8

    def clear(i, c):
        for array in (field, other):
            array[i, pl.ds(0, 8), :] = zero
            array[i, pl.ds(slices + 16, 8), :] = zero
        return c

    lax.fori_loop(0, total, clear, 0)
    flux_slices[pl.ds(0, 8), :] = zero
    own = pl.multiple_of(base, 8)
    beyond = pl.multiple_of(8 + slices * (1 - cut), 8)
    field[pl.ds(HALO, rows), pl.ds(own, slices), :] = relaxed[...]
    for copy in copies:
        copy.wait_recv()
    above = (here > 0).astype(F32)
    below = (here < last).astype(F32)
    field[pl.ds(HALO, rows), pl.ds(beyond, 8), :] = side[1]
    field[pl.ds(0, HALO), pl.ds(own, slices), :] = edge[2].astype(F32) * above
    field[pl.ds(0, HALO), pl.ds(beyond, 8), :] = corner[0] * above
    field[pl.ds(HALO + rows, HALO), pl.ds(own, slices), :] = edge[3].astype(F32) * below
    field[pl.ds(HALO + rows, HALO), pl.ds(beyond, 8), :] = corner[1] * below

    lane = lax.broadcasted_iota(jnp.int32, (8, cols), 1)
    not_last = lane < cols - 1
    not_first = lane > 0
    first_row = here * rows - HALO
    row_limit = (last + 1) * rows

    def sweep(old, new, low, high):
        def row_body(r, store):
            inside = jnp.logical_and(first_row + r >= 0, first_row + r < row_limit).astype(F32)
            for chunk in range(chunks):
                at = 8 + 8 * chunk
                value = old[r, at : at + 8, :]
                rise_rows = old[r + 1, at : at + 8, :] - value
                rise_slices = old[r, at + 1 : at + 9, :] - value
                rise_cols = jnp.where(not_last, pltpu.roll(value, cols - 1, 1), 0.0) - value
                square = rise_rows * rise_rows + rise_cols * rise_cols + rise_slices * rise_slices
                scale = lax.rsqrt(smooth_square + square) * inside
                along_rows = rise_rows * scale
                if store:
                    along_cols = rise_cols * scale
                    along_slices = rise_slices * scale
                    flux_slices[at : at + 8, :] = along_slices
                    diverge = along_rows - flux_rows[at : at + 8, :]
                    before = jnp.where(not_first, pltpu.roll(along_cols, 1, 1), 0.0)
                    diverge = diverge + (along_cols - before)
                    diverge = diverge + (along_slices - flux_slices[at - 1 : at + 7, :])
                    new[r, at : at + 8, :] = (value + flow_step * diverge) * inside
                flux_rows[at : at + 8, :] = along_rows

        row_body(low - 1, False)

        def body(r, c):
            row_body(r, True)
            return c

        lax.fori_loop(low, high, body, 0)

    pair = (field, other)
    for repeat in range(SWEEPS):
        sweep(pair[repeat % 2], pair[(repeat + 1) % 2], 1 + repeat, total - 1 - repeat)
    final = pair[SWEEPS % 2]

    def finish(r, c):
        out[r] = final[r + HALO, pl.ds(own, slices), :].T
        return c

    lax.fori_loop(0, rows, finish, 0)
    for copy in copies:
        copy.wait_send()


def smooth(relaxed):
    rows, slices, cols = relaxed.shape
    tall = slices + 24
    return pl.pallas_call(
        sweep_kernel,
        out_shape=jax.ShapeDtypeStruct((rows, cols, slices), F32),
        in_specs=[pl.BlockSpec(memory_space=pltpu.VMEM)],
        out_specs=pl.BlockSpec(memory_space=pltpu.VMEM),
        scratch_shapes=[
            pltpu.VMEM((rows + 2 * HALO, tall, cols), F32),
            pltpu.VMEM((rows + 2 * HALO, tall, cols), F32),
            pltpu.VMEM((tall, cols), F32),
            pltpu.VMEM((tall, cols), F32),
            pltpu.VMEM((4, HALO, slices, cols), BF16),
            pltpu.VMEM((2, rows, 8, cols), F32),
            pltpu.VMEM((2, HALO, 8, cols), F32),
            pltpu.SemaphoreType.DMA((2,)),
            pltpu.SemaphoreType.DMA((2,)),
            pltpu.SemaphoreType.DMA((3,)),
            pltpu.SemaphoreType.DMA((3,)),
        ],
        compiler_params=pltpu.CompilerParams(
            collective_id=1, has_side_effects=True, vmem_limit_bytes=VMEM_LIMIT
        ),
        name="smooth",
    )(relaxed)


def per_device(image, weights, tiles, blocks, owners, count, measured):
    partial = forward(tiles, blocks, owners, count, image, weights)
    residual, spread = exchange(partial, measured)
    relaxed = backward(tiles, blocks, owners, count, image, spread, weights)
    return smooth(relaxed), residual


def solution(mesh):
    placed = (
        P("plane", None, "cuts"),
        P("plane", None, None),
        P("plane"),
        P("plane"),
        P(),
        P("plane"),
        P("plane", None, "cuts"),
    )
    return jax.shard_map(
        per_device,
        mesh=mesh,
        in_specs=placed,
        out_specs=(P("plane", None, "cuts"), P("plane", None, "cuts")),
        check_vma=False,
    )
```

```python
import functools

import jax
import jax.numpy as jnp
from jax import lax
from jax.experimental import pallas as pl
from jax.experimental.pallas import tpu as pltpu
from jax.sharding import PartitionSpec as P

TILE = 16
SWEEPS = 4
smooth_square = 0.09
flow_step = 0.04
relax_step = 4.0

SIDE = 4
HALO = 4
CHUNKS = 4
MIB = 1024 * 1024
ORDERS = ((0, 1, 2), (1, 2, 0), (2, 0, 1))
STREAMS = tuple((i % 3, 16 * i, 16) for i in range(8))

F32 = jnp.float32
BF16 = jnp.bfloat16


def coordinates():
    here = lax.axis_index("plane")
    return here // (SIDE * SIDE), (here // SIDE) % SIDE, here % SIDE


def relative_slot(owner):
    x, y, z = coordinates()
    dx = lax.bitwise_and(owner // (SIDE * SIDE) - x + SIDE, SIDE - 1)
    dy = lax.bitwise_and((owner // SIDE) % SIDE - y + SIDE, SIDE - 1)
    dz = lax.bitwise_and(owner % SIDE - z + SIDE, SIDE - 1)
    return (dx * SIDE + dy) * SIDE + dz


def forward_kernel(*refs):
    tables, (count, image, weights, out, held, rows, voxels, sums, arrived) = refs[:3], refs[3:12]
    tiles, blocks, owners, ready = refs[12:]
    slots = sums.shape[0] - 1
    chunks = arrived.shape[0]
    width = held.shape[0] // chunks

    def load(c):
        part = pl.ds(c * width, width)
        return pltpu.make_async_copy(weights.at[part], held.at[part], arrived.at[c])

    early = [pltpu.make_async_copy(image, rows, ready.at[3])]
    for i, (table, local) in enumerate(zip(tables, refs[12:15])):
        early.append(pltpu.make_async_copy(table, local, ready.at[i]))
    for copy in early:
        copy.start()
    for c in range(chunks):
        load(c).start()

    def clear(i, c):
        sums[i] = jnp.zeros(sums.shape[1:], F32)
        return c

    lax.fori_loop(0, slots, clear, 0)
    for copy in early:
        copy.wait()
    for tile in range(voxels.shape[0]):
        piece = rows[:, tile * TILE : (tile + 1) * TILE, :]
        voxels[tile] = piece.reshape(TILE * TILE, piece.shape[-1]).T.astype(BF16)

    def chunk(c, carry):
        load(c).wait()
        for i in range(width):
            pair = c * width + i
            slot = jnp.where(pair < count[0], relative_slot(owners[blocks[pair]]), slots)
            product = jnp.dot(voxels[tiles[pair]], held[pair], preferred_element_type=F32)
            sums[slot, 0] += product[:, :128]
            sums[slot, 1] += product[:, 128:]
        return carry

    lax.fori_loop(0, chunks, chunk, 0)

    def finish(i, c):
        out[i] = sums[i].astype(BF16)
        return c

    lax.fori_loop(0, slots, finish, 0)


def smem():
    return pl.BlockSpec(memory_space=pltpu.SMEM)


def vmem():
    return pl.BlockSpec(memory_space=pltpu.VMEM)


def forward(*operands):
    owners, _, image, weights = operands[2:]
    pairs, voxels, rays = weights.shape
    rows, cols, slices = image.shape
    slots = owners.shape[0]
    operands = [
        x if i == 3 else pltpu.with_memory_space_constraint(x, pltpu.HBM)
        for i, x in enumerate(operands)
    ]
    hbm = pl.BlockSpec(memory_space=pltpu.HBM)
    return pl.pallas_call(
        forward_kernel,
        out_shape=jax.ShapeDtypeStruct((slots, 2, slices, 128), BF16),
        in_specs=[hbm, hbm, hbm, smem(), hbm, hbm],
        out_specs=vmem(),
        scratch_shapes=[
            pltpu.VMEM((pairs, voxels, rays), BF16),
            pltpu.VMEM((rows, cols, slices), F32),
            pltpu.VMEM((cols // TILE, slices, voxels), BF16),
            pltpu.VMEM((slots + 1, 2, slices, 128), F32),
            pltpu.SemaphoreType.DMA((CHUNKS,)),
            *[pltpu.SMEM(x.shape, jnp.int32) for x in operands[:3]],
            pltpu.SemaphoreType.DMA((4,)),
        ],
        compiler_params=pltpu.CompilerParams(vmem_limit_bytes=30 * MIB),
        name="project",
    )(*operands)


def backward_kernel(tiles, blocks, owners, count, image, spread, weights, out, sums):
    tile_count = sums.shape[0] - 1
    width = weights.shape[0] // CHUNKS
    for i in range(tile_count):
        sums[i] = jnp.zeros(sums.shape[1:], F32)

    def chunk(c, carry):
        for i in range(width):
            pair = c * width + i
            tile = jnp.where(pair < count[0], tiles[pair], tile_count)
            slot = relative_slot(owners[blocks[pair]])
            values = jnp.concatenate([spread[slot, 0], spread[slot, 1]], axis=1)
            sums[tile] += lax.dot_general(
                values, weights[pair], (((1,), (1,)), ((), ())), preferred_element_type=F32
            )
        return carry

    lax.fori_loop(0, CHUNKS, chunk, 0)
    rows, cols, slices = image.shape
    for tile in range(tile_count):
        here = slice(tile * TILE, (tile + 1) * TILE)
        update = sums[tile].T.reshape(rows, TILE, slices)
        out[:, here, :] = jnp.maximum(image[:, here, :] + relax_step * update, 0.0)


def backward(tiles, blocks, owners, count, image, spread, weights):
    pairs, voxels, rays = weights.shape
    rows, cols, slices = image.shape
    return pl.pallas_call(
        backward_kernel,
        out_shape=jax.ShapeDtypeStruct((rows, cols, slices), F32),
        in_specs=[smem(), smem(), smem(), smem(), vmem(), vmem(), vmem()],
        out_specs=vmem(),
        scratch_shapes=[pltpu.VMEM((cols // TILE + 1, slices, voxels), F32)],
        compiler_params=pltpu.CompilerParams(vmem_limit_bytes=24 * MIB),
        name="backproject",
    )(tiles, blocks, owners, count, image, spread, weights)


def neighbour(dim, shift):
    place = list(coordinates())
    place[dim] = (place[dim] + shift + SIDE) % SIDE
    return (place[0] * SIDE + place[1]) * SIDE + place[2]


def pick(order, *where):
    index = [slice(None)] * 3
    for position, value in enumerate(where):
        index[ORDERS[order][position]] = value
    return tuple(index)


def exchange_kernel(partial, measured, residual, gather, wanted, own, buffers, sems):
    sum_send, sum_recv, spread_send, spread_recv = sems

    barrier = pltpu.get_barrier_semaphore()
    for dim in range(3):
        for shift in (1, 2, 3):
            pl.semaphore_signal(barrier, inc=1, device_id={"plane": neighbour(dim, shift)})
    for half in range(2):
        wanted[half] = measured[0, half * 128 : (half + 1) * 128, :].T
    pl.semaphore_wait(barrier, 9)
    sends = []

    def combine(target, first, *others):
        def one(index):
            value = first[index].astype(F32)
            for other in others:
                value = value + other[index].astype(F32)
            target[index] = value.astype(target.dtype)

        blocks = target.shape[:-2]
        if len(blocks) == 2:

            def body(i, c):
                for k in range(blocks[1]):
                    one((i, k))
                return c

            lax.fori_loop(0, blocks[0], body, 0)
        elif len(blocks) == 1:
            for k in range(blocks[0]):
                one((k,))
        else:
            one((slice(None),))

    def stages(number):
        order, first, rows = STREAMS[number]
        part_rows = pl.ds(first, rows)
        opposite, direct, nearest, late, middle, total = buffers[number]

        def source(phase, j, half):
            if phase == 0:
                return partial.at[pick(order, j) + (half, part_rows)]
            return middle.at[pick(order, 0, j) + (half,)]

        def send(pool, slot, phase, src, dst, shift):
            copy = pltpu.make_async_remote_copy(
                src_ref=src,
                dst_ref=dst,
                send_sem=pool[0].at[number, slot],
                recv_sem=pool[1].at[number, slot],
                device_id={"plane": neighbour(ORDERS[order][phase], shift)},
            )
            copy.start()
            sends.append(copy)
            return copy

        adding = (sum_send, sum_recv)
        spreading = (spread_send, spread_recv)
        state = {}

        def sum_early(phase):
            opp, dirs = opposite[phase], direct[phase]
            state["opp"] = [
                send(adding, 6 * phase, phase, source(phase, 2, 0), opp.at[0], 1),
                send(adding, 6 * phase + 1, phase, source(phase, 2, 1), opp.at[1], -1),
            ]
            state["dir"] = [
                send(adding, 6 * phase + 2, phase, source(phase, 1, 1), dirs.at[0, 1], 1),
                send(adding, 6 * phase + 3, phase, source(phase, 3, 0), dirs.at[1, 0], -1),
            ]

        def sum_late(phase):
            opp, dirs = opposite[phase], direct[phase]
            for half, (j, shift) in enumerate(((1, 1), (3, -1))):
                state["opp"][half].wait_recv()
                here = source(phase, j, half)
                joined = late.at[half] if phase == 0 else here
                combine(joined, here, opp.at[half])
                state["dir"].append(
                    send(adding, 6 * phase + 4 + half, phase, joined, dirs.at[half, half], shift)
                )

        def sum_end(phase):
            dirs = direct[phase]
            for copy in state["dir"]:
                copy.wait_recv()
            for half in range(2):
                if phase == 0:
                    target = middle.at[pick(order, 0) + (half,)]
                else:
                    target = total.at[:, half]
                combine(target, source(phase, 0, half), dirs.at[0, half], dirs.at[1, half])

        def sum_nearest():
            state["near"] = [
                send(adding, 11 + j, 2, total.at[j], nearest.at[j - 1], j) for j in (2, 1, 3)
            ]

        def settle():
            for copy in state["near"]:
                copy.wait_recv()
            for half in range(2):
                reached = total[0, half]
                for i in range(3):
                    reached = reached + nearest[i, half]
                mismatch = wanted[half, part_rows] - reached
                value = (mismatch * lax.rsqrt(1.0 + mismatch * mismatch)).astype(BF16)
                own[half, part_rows] = value.astype(F32)
                gather[0, 0, 0, half, part_rows] = value

        def held(phase, j, *half):
            index = pick(order, *([0] * phase), j)
            return gather.at[index + ((half[0] if half else slice(None)), part_rows)]

        def spread_nearest():
            state["near"] = [
                send(spreading, 7 + j, 2, held(2, 0), held(2, SIDE - j), j) for j in (2, 1, 3)
            ]

        def spread_met():
            for copy in state["near"]:
                copy.wait_recv()

        def spread_early(phase):
            slot = 4 * phase
            state["one"] = [
                send(spreading, slot, phase, held(phase, 0), held(phase, 3), 1),
                send(spreading, slot + 1, phase, held(phase, 0), held(phase, 1), -1),
            ]

        def spread_late(phase):
            slot = 4 * phase + 2
            state["two"] = []
            for half, (j, shift) in enumerate(((3, 1), (1, -1))):
                state["one"][half].wait_recv()
                state["two"].append(
                    send(spreading, slot + half, phase, held(phase, j, half), held(phase, 2, half), shift)
                )

        def spread_end(phase):
            for copy in state["two"]:
                copy.wait_recv()

        def together(*steps):
            def run():
                for step, *args in steps:
                    step(*args)

            return run

        return [
            together((sum_early, 0)),
            together((sum_late, 0)),
            together((sum_end, 0), (sum_early, 1)),
            together((sum_late, 1)),
            together((sum_end, 1), (sum_nearest,)),
            together((settle,), (spread_nearest,)),
            together((spread_met,), (spread_early, 1)),
            together((spread_late, 1)),
            together((spread_end, 1), (spread_early, 0)),
            together((spread_late, 0)),
            together((spread_end, 0)),
        ]

    plan = []
    for number in range(len(STREAMS)):
        for k, run in enumerate(stages(number)):
            plan.append((k, number, run))
    plan.sort(key=lambda entry: entry[:2])
    for _, _, run in plan:
        run()

    for half in range(2):
        residual[0, half * 128 : (half + 1) * 128, :] = own[half].T.astype(BF16)
    for copy in sends:
        copy.wait_send()


def exchange(partial, measured):
    slots, halves, slices, lanes = partial.shape
    rays = measured.shape[1]
    cube = (SIDE, SIDE, SIDE)
    count = len(STREAMS)
    buffers = []
    for order, _, rows in STREAMS:
        for blocks in ((SIDE, SIDE), (SIDE,)):
            buffers.append(pltpu.VMEM((2, *blocks, rows, lanes), BF16))
        for blocks in ((SIDE, SIDE), (SIDE,)):
            buffers.append(pltpu.VMEM((2, 2, *blocks, rows, lanes), BF16))
        thin = [1 if dim == ORDERS[order][0] else SIDE for dim in range(3)]
        buffers.append(pltpu.VMEM((3, halves, rows, lanes), F32))
        buffers.append(pltpu.VMEM((2, SIDE, SIDE, rows, lanes), BF16))
        buffers.append(pltpu.VMEM((*thin, halves, rows, lanes), BF16))
        buffers.append(pltpu.VMEM((SIDE, halves, rows, lanes), F32))
    each = len(buffers) // count

    def kernel(partial, measured, residual, gather, wanted, own, *rest):
        grouped = []
        for i in range(count):
            mine = rest[each * i : each * (i + 1)]
            grouped.append((mine[0:2], mine[2:4], *mine[4:]))
        exchange_kernel(
            partial, measured, residual, gather, wanted, own, grouped, rest[each * count :]
        )

    residual, spread = pl.pallas_call(
        kernel,
        out_shape=(
            jax.ShapeDtypeStruct((1, rays, slices), BF16),
            jax.ShapeDtypeStruct((*cube, halves, slices, lanes), BF16),
        ),
        in_specs=[vmem(), vmem()],
        out_specs=(vmem(), vmem()),
        scratch_shapes=[
            pltpu.VMEM((halves, slices, lanes), F32),
            pltpu.VMEM((halves, slices, lanes), F32),
            *buffers,
            pltpu.SemaphoreType.DMA((count, 15)),
            pltpu.SemaphoreType.DMA((count, 15)),
            pltpu.SemaphoreType.DMA((count, 11)),
            pltpu.SemaphoreType.DMA((count, 11)),
        ],
        compiler_params=pltpu.CompilerParams(
            collective_id=0, has_side_effects=True, vmem_limit_bytes=24 * MIB
        ),
        name="exchange",
    )(partial.reshape(*cube, halves, slices, lanes), measured)
    return residual, spread.reshape(slots, halves, slices, lanes)


def sweep_kernel(image, out, relaxed, field, other, flux_rows, flux_slices, edge, side, corner, *sems):
    row_send, row_recv, side_send, side_recv = sems
    rows, slices, cols = relaxed.shape
    here = lax.axis_index("plane")
    cut = lax.axis_index("cuts")
    last = lax.axis_size("plane") - 1
    up = (here + last) % (last + 1)
    down = (here + 1) % (last + 1)
    base = 8 + 8 * cut

    def turn(r, c):
        relaxed[r] = image[r].T
        return c

    barrier = pltpu.get_barrier_semaphore()
    for plane in (up, down):
        for core in (0, 1):
            pl.semaphore_signal(barrier, inc=1, device_id={"plane": plane, "cuts": core})
    pl.semaphore_signal(barrier, inc=1, device_id={"plane": here, "cuts": 1 - cut})
    lax.fori_loop(0, rows, turn, 0)
    pl.semaphore_wait(barrier, 5)

    edge[0] = relaxed[rows - HALO :].astype(BF16)
    edge[1] = relaxed[:HALO].astype(BF16)
    start = pl.multiple_of(120 * (1 - cut), 8)
    side[0] = relaxed[:, pl.ds(start, 8), :]
    copies = []

    def send(src, dst, plane, core, number, which):
        copy = pltpu.make_async_remote_copy(
            src_ref=src,
            dst_ref=dst,
            send_sem=which[0].at[number],
            recv_sem=which[1].at[number],
            device_id={"plane": plane, "cuts": core},
        )
        copy.start()
        copies.append(copy)

    send(side.at[0], side.at[1], here, 1 - cut, 0, (side_send, side_recv))
    send(side.at[0, pl.ds(rows - HALO, HALO)], corner.at[0], down, 1 - cut, 1, (side_send, side_recv))
    send(side.at[0, pl.ds(0, HALO)], corner.at[1], up, 1 - cut, 2, (side_send, side_recv))
    send(edge.at[0], edge.at[2], down, cut, 0, (row_send, row_recv))
    send(edge.at[1], edge.at[3], up, cut, 1, (row_send, row_recv))

    total = rows + 2 * HALO
    zero = jnp.zeros((8, cols), F32)
    chunks = (slices + 8) // 8

    def clear(i, c):
        for array in (field, other):
            array[i, pl.ds(0, 8), :] = zero
            array[i, pl.ds(slices + 16, 8), :] = zero
        return c

    lax.fori_loop(0, total, clear, 0)
    for i in range(2):
        flux_slices[i, pl.ds(0, 8), :] = zero
    own = pl.multiple_of(base, 8)
    beyond = pl.multiple_of(8 + slices * (1 - cut), 8)
    field[pl.ds(HALO, rows), pl.ds(own, slices), :] = relaxed[...]
    copies[0].wait_recv()
    field[pl.ds(HALO, rows), pl.ds(beyond, 8), :] = side[1]

    lane = lax.broadcasted_iota(jnp.int32, (8, cols), 1)
    not_last = lane < cols - 1
    not_first = lane > 0
    first_row = here * rows - HALO
    row_limit = (last + 1) * rows

    def sweep(old, new, low, high, edge_rows):
        def weight(r):
            if not edge_rows:
                return flow_step
            inside = jnp.logical_and(first_row + r >= 0, first_row + r < row_limit)
            return jnp.where(inside, flow_step, 0.0)

        def flux(r, at, value, below, step):
            rise_rows = below - value
            rise_slices = old[r, at + 1 : at + 9, :] - value
            rise_cols = jnp.where(not_last, pltpu.roll(value, cols - 1, 1), 0.0) - value
            square = rise_rows * rise_rows + rise_cols * rise_cols + rise_slices * rise_slices
            scale = lax.rsqrt(smooth_square + square) * step
            return rise_rows * scale, rise_cols * scale, rise_slices * scale

        step = weight(low - 1)
        for chunk in range(chunks):
            at = 8 + 8 * chunk
            value = old[low - 1, at : at + 8, :]
            flux_rows[at : at + 8, :] = flux(low - 1, at, value, old[low, at : at + 8, :], step)[0]

        def body(i, c):
            r = low + 2 * i
            steps = (weight(r), weight(r + 1))
            for chunk in range(chunks):
                at = 8 + 8 * chunk
                here_rows = [old[r + k, at : at + 8, :] for k in range(3)]
                passed = flux_rows[at : at + 8, :]
                for k in range(2):
                    value = here_rows[k]
                    along_rows, along_cols, along_slices = flux(
                        r + k, at, value, here_rows[k + 1], steps[k]
                    )
                    flux_slices[k, at : at + 8, :] = along_slices
                    before = jnp.where(not_first, pltpu.roll(along_cols, 1, 1), 0.0)
                    diverge = (along_rows - passed) + (along_cols - before)
                    diverge = diverge + (along_slices - flux_slices[k, at - 1 : at + 7, :])
                    new[r + k, at : at + 8, :] = value + diverge
                    passed = along_rows
                flux_rows[at : at + 8, :] = passed
            return c

        lax.fori_loop(0, (high - low) // 2, body, 0)

    pair = (field, other)
    for repeat in range(SWEEPS):
        old, new = pair[repeat % 2], pair[(repeat + 1) % 2]
        sweep(old, new, HALO + 1 + repeat, HALO + rows - 1 - repeat, False)

    above = (here > 0).astype(F32)
    below = (here < last).astype(F32)
    for copy in copies[1:]:
        copy.wait_recv()
    field[pl.ds(0, HALO), pl.ds(own, slices), :] = edge[2].astype(F32) * above
    field[pl.ds(0, HALO), pl.ds(beyond, 8), :] = corner[0] * above
    field[pl.ds(HALO + rows, HALO), pl.ds(own, slices), :] = edge[3].astype(F32) * below
    field[pl.ds(HALO + rows, HALO), pl.ds(beyond, 8), :] = corner[1] * below
    for repeat in range(SWEEPS):
        old, new = pair[repeat % 2], pair[(repeat + 1) % 2]
        sweep(old, new, 1 + repeat, HALO + 1 + repeat, True)
        sweep(old, new, HALO + rows - 1 - repeat, 2 * HALO + rows - 1 - repeat, True)
        if repeat < SWEEPS - 1:
            new[HALO + rows] = new[HALO + rows] * below
    final = pair[SWEEPS % 2]

    def finish(r, c):
        out[r] = final[r + HALO, pl.ds(own, slices), :].T
        return c

    lax.fori_loop(0, rows, finish, 0)
    for copy in copies:
        copy.wait_send()


def smooth(relaxed):
    rows, cols, slices = relaxed.shape
    tall = slices + 24
    return pl.pallas_call(
        sweep_kernel,
        out_shape=jax.ShapeDtypeStruct((rows, cols, slices), F32),
        in_specs=[pl.BlockSpec(memory_space=pltpu.VMEM)],
        out_specs=pl.BlockSpec(memory_space=pltpu.VMEM),
        scratch_shapes=[
            pltpu.VMEM((rows, slices, cols), F32),
            pltpu.VMEM((rows + 2 * HALO, tall, cols), F32),
            pltpu.VMEM((rows + 2 * HALO, tall, cols), F32),
            pltpu.VMEM((tall, cols), F32),
            pltpu.VMEM((2, tall, cols), F32),
            pltpu.VMEM((4, HALO, slices, cols), BF16),
            pltpu.VMEM((2, rows, 8, cols), F32),
            pltpu.VMEM((2, HALO, 8, cols), F32),
            pltpu.SemaphoreType.DMA((2,)),
            pltpu.SemaphoreType.DMA((2,)),
            pltpu.SemaphoreType.DMA((3,)),
            pltpu.SemaphoreType.DMA((3,)),
        ],
        compiler_params=pltpu.CompilerParams(
            collective_id=1, has_side_effects=True, vmem_limit_bytes=20 * MIB
        ),
        name="smooth",
    )(relaxed)


def per_device(image, weights, tiles, blocks, owners, count, measured):
    partial = forward(tiles, blocks, owners, count, image, weights)
    partial, weights = lax.optimization_barrier((partial, weights))
    residual, spread = exchange(partial, measured)
    relaxed = backward(tiles, blocks, owners, count, image, spread, weights)
    return smooth(relaxed), residual


def solution(mesh):
    placed = (
        P("plane", None, "cuts"),
        P("plane", None, None),
        P("plane"),
        P("plane"),
        P(),
        P("plane"),
        P("plane", None, "cuts"),
    )
    return jax.shard_map(
        per_device,
        mesh=mesh,
        in_specs=placed,
        out_specs=(P("plane", None, "cuts"), P("plane", None, "cuts")),
        check_vma=False,
    )
```
